512 devices in a mesh: grp: 16 (over x_hi, y), sub: 32 (over z, x_lo, core).
Axes of the slice: x: 4 (x_hi: 2, x_lo: 2; x = x_hi * 2 + x_lo), y: 8, z: 8, core: 2. Of those that a mesh axis runs over, the one named last changes fastest.
Arguments:
- control: float32 [16, 32, 384, 768], P('grp', None, 'sub'), may hold values from -6 to 6
- perturbation: float32 [16, 32, 384, 768], P('grp', None, 'sub'), may hold values from -6 to 6
- weight: float32 [32, 384, 768], P('grp', 'sub'), may hold values from 0.25 to 2
- half_width: int32 [384], replicated, may hold values from 1 to 12, as said below
Outputs:
- increment: float32 [32, 384, 768], P('grp', 'sub')
- adjoint: float32 [16, 32, 384, 768], P('grp', None, 'sub')
The draws below stay inside these ranges and needn't reach their ends.
Inputs may be any that keep to these rules, and one draw needn't show every extreme that they name: `half_width`: at least one latitude has half-width 12.
All inputs are finite; a program needn't handle non-finite values.
Results may differ from the reference program's by a relative error of at most 0.0001.
Values sent between devices are 32-bit elements; how exact they have to be, the bound alone decides.
A program may use at most 64 MiB of HBM per device.

```python
import math
import jax
import jax.numpy as jnp
from jax import lax

LAT = 384
LON = 768
HWMAX = 12
LEVELS = 32
MEMBERS = 16


def draw_half_width(key, part):
    values = jax.random.randint(jax.random.fold_in(key, 11), (LAT,), 1, HWMAX + 1)
    where_max = jax.random.randint(jax.random.fold_in(key, 23), (), 0, LAT)
    positions = jnp.arange(LAT, dtype=jnp.int32)
    return jnp.where(positions == where_max, HWMAX, values).astype(jnp.int32)


def with_spikes(values, own_key, source, target, blocks, factor):
    owner, partner = [(jnp.arange(values.shape[axis_at]) // (values.shape[axis_at] // blocks)).reshape([-1 if axis == axis_at else 1 for axis in range(values.ndim)]) for axis_at in (source, target)]
    chosen = jax.random.permutation(own_key, blocks)[partner]
    strong = (owner == chosen) | (owner == (partner + blocks // 2) % blocks)
    return jnp.where(strong, factor * values, values)


def shard_levels(own_key, shape, cuts, smallest, top_value):
    factor_of = 1.0
    for axis_at, parts in cuts:
        steps = jax.random.uniform(jax.random.fold_in(jax.random.fold_in(own_key, 6), axis_at), (parts,), jnp.float32, smallest / len(cuts), top_value / len(cuts))
        factor_of = factor_of * jnp.repeat(jnp.exp(steps), shape[axis_at] // parts).reshape((-1,) + (1,) * (len(shape) - 1 - axis_at))
    return factor_of


def gaussian(stream_key, extent, scale, reach, split=(), kind=jnp.bfloat16):
    gain = shard_levels(stream_key, extent, split, -0.22, 0.18) if split else 1.0
    drawn = jax.random.normal(stream_key, extent, jnp.float32) * scale * gain
    return jnp.minimum(jnp.maximum(drawn, -reach), reach).astype(kind)


def gaussian_with(own_key, extent, deviation, bound, split, heavy, kind=jnp.bfloat16):
    drawn = deviation * jax.random.normal(own_key, extent, jnp.float32)
    if split:
        drawn = drawn * shard_levels(own_key, extent, split, -0.22, 0.18)
    return jnp.clip(with_spikes(drawn, jax.random.fold_in(own_key, 3), *heavy), -bound, bound).astype(kind)


def setup_inputs(seed: int = 0) -> dict:
    key_list = jax.random.split(jax.random.key(seed), 5)
    return {
        "control": gaussian(key_list[0], (MEMBERS, LEVELS, LAT, LON), 1.0, 6.0, ((0, 16), (2, 32)), jnp.float32),
        "perturbation": gaussian_with(key_list[1], (MEMBERS, LEVELS, LAT, LON), 1.0, 6.0, ((0, 16), (2, 32)), (0, 1, 16, 2.0), jnp.float32),
        "weight": jnp.clip(jnp.exp(math.log(2.0) - 2.0794415 * jax.random.uniform(key_list[2], (LEVELS, LAT, LON), jnp.float32) ** shard_levels(key_list[2], (LEVELS, LAT, LON), ((0, 16), (1, 32)), -0.2, 0.2)), 0.25, 2.0),
        "half_width": draw_half_width(jax.random.fold_in(key_list[4], 71), 0),
    }


lon_sigma = 4.0
lon_reach = 12.0


def lat_matrix(half_width):
    length = half_width.shape[0]
    row_index = jnp.arange(length, dtype=jnp.int32)[:, None]
    col_index = jnp.arange(length, dtype=jnp.int32)[None, :]
    offset = (row_index - col_index).astype(jnp.float32)
    reach_rows = half_width.astype(jnp.float32)[:, None]
    spread_width = 0.5 * reach_rows + 0.5
    inside = jnp.abs(offset) <= reach_rows
    kernel = jnp.where(inside, jnp.exp(-0.5 * (offset / spread_width) ** 2), jnp.zeros_like(offset))
    return kernel / jnp.sum(kernel, axis=1, keepdims=True)


def lon_matrix(length):
    row_index = jnp.arange(length, dtype=jnp.int32)[:, None]
    col_index = jnp.arange(length, dtype=jnp.int32)[None, :]
    offset = (row_index - col_index) % length
    offset = jnp.where(offset * 2 > length, offset - length, offset).astype(jnp.float32)
    inside = jnp.abs(offset) <= lon_reach
    kernel = jnp.where(inside, jnp.exp(-0.5 * (offset / lon_sigma) ** 2), jnp.zeros_like(offset))
    return kernel / jnp.sum(kernel, axis=1, keepdims=True)


def filter_forward(field_in, lat_filter, lon_filter):
    halfway = jnp.einsum('ij,ljk->lik', lat_filter, field_in, precision=lax.Precision.HIGHEST)
    return jnp.einsum('lik,mk->lim', halfway, lon_filter, precision=lax.Precision.HIGHEST)


def filter_adjoint(field_in, lat_filter, lon_filter):
    halfway = jnp.einsum('ji,ljk->lik', lat_filter, field_in, precision=lax.Precision.HIGHEST)
    return jnp.einsum('lik,km->lim', halfway, lon_filter, precision=lax.Precision.HIGHEST)


def reference(control, perturbation, weight, half_width):
    lat_filter = lat_matrix(half_width)
    lon_filter = lon_matrix(control.shape[3])

    def add_member(summed, pieces):
        member_control, member_pert = pieces
        return summed + member_pert * filter_forward(member_control, lat_filter, lon_filter), None

    summed, unused = lax.scan(add_member, jnp.zeros(control.shape[1:], jnp.float32), (control, perturbation))
    increment = weight * summed

    def one_member(member_pert):
        return filter_adjoint(member_pert * increment, lat_filter, lon_filter)

    adjoint = lax.map(one_member, perturbation)
    return increment, adjoint
```

```python
import functools
import math

import jax
import jax.numpy as jnp
from jax import lax
from jax.experimental import pallas as pl
from jax.experimental.pallas import tpu as pltpu
from jax.sharding import PartitionSpec as P

MESH = pl.DeviceIdType.MESH
ROWS = 12
TILE = 8
CHUNKS = 4
LON = 768
HALF = 384
RING = 8
TAPS = 2 * ROWS + 1
PAD = 12
REACH = 12
LON_SUM = sum(math.exp(-0.5 * (d / 4.0) ** 2) for d in range(-REACH, REACH + 1))
WINDOW = 512
OUT = 256


def kernel(
    n_sub,
    hw,
    control,
    pert,
    weight,
    inc_out,
    adj_out,
    cbuf,
    pbuf,
    ybuf,
    lhs_hi,
    lhs_lo,
    f_hi,
    f_lo,
    wtab,
    prod,
    rs_f,
    rs_b,
    tot,
    xin,
    wpart,
    wbuf,
    wfull,
    inc,
    own,
    to_l,
    to_r,
    from_l,
    from_r,
    incst,
    c_send,
    c_recv,
    load_sem,
    rsf_send,
    rsf_recv,
    rsb_send,
    rsb_recv,
    x_send,
    x_recv,
    ag_send,
    ag_recv,
    a_send,
    a_recv,
    w_send,
    w_recv,
    out_sem,
):
    g = lax.axis_index("grp")
    s = lax.axis_index("sub")
    y = lax.rem(g, RING)
    xh = lax.div(g, RING)
    base = xh * RING
    core = lax.rem(s, 2)
    sign = 1 - 2 * core
    left = lax.rem(s + n_sub - 1, n_sub)
    right = lax.rem(s + 1, n_sub)

    def ring(offset):
        return lax.rem(y + sign * offset + RING, RING)

    ahead = base + ring(1)
    behind = base + ring(-1)
    partner = (1 - xh) * RING + y

    def remote(src, dst, ss, rs, grp, sub):
        return pltpu.make_async_remote_copy(
            src_ref=src, dst_ref=dst, send_sem=ss, recv_sem=rs, device_id=(grp, sub), device_id_type=MESH
        )

    pending = []

    def launch(copy):
        copy.start()
        pending.append(copy)
        return copy

    loads = {}
    for k in range(CHUNKS):
        levels = pl.ds(k * TILE, TILE)
        loads["c", k] = pltpu.make_async_copy(control.at[:, levels, :], cbuf.at[k, pl.ds(ROWS, ROWS)], load_sem.at[0, k])
        loads["p", k] = pltpu.make_async_copy(pert.at[:, levels, :], pbuf.at[k], load_sem.at[1, k])
        loads["c", k].start()
        loads["p", k].start()

    def weight_piece(ref, owner):
        rows = pl.ds(3 * lax.div(owner, 2), 3)
        cols = pl.ds(pl.multiple_of(lax.rem(owner, 2) * HALF, 128), HALF)
        return ref.at[rows, :, cols]

    loads["w"] = pltpu.make_async_copy(weight_piece(weight, y), wbuf.at[g], load_sem.at[2, 0])
    loads["w"].start()

    barrier = pltpu.get_barrier_semaphore()
    for grp, sub in ((g, left), (g, right), (ahead, s), (behind, s), (partner, s)):
        pl.semaphore_signal(barrier, inc=1, device_id=(grp, sub), device_id_type=MESH)
    pl.semaphore_wait(barrier, 5)

    halos = {}

    def send_control(k):
        src = control.at[:, pl.ds(k * TILE, TILE), :]
        halos["c", k] = (
            launch(remote(src, cbuf.at[k, pl.ds(0, ROWS)], c_send.at[k, 0], c_recv.at[k, 0], g, right)),
            launch(remote(src, cbuf.at[k, pl.ds(2 * ROWS, ROWS)], c_send.at[k, 1], c_recv.at[k, 1], g, left)),
        )

    send_control(0)
    send_control(1)
    halos["w"] = launch(remote(weight, wpart, w_send.at[0], w_recv.at[0], partner, s))

    def fill(r, carry):
        row = s * ROWS + r
        reach = jnp.full((8, 128), hw[row].astype(jnp.float32))
        spread = 0.5 * reach + 0.5
        values = []
        for d in range(ROWS + 1):
            e = jnp.exp(-0.5 * (d / spread) ** 2)
            values.append(jnp.where(d <= reach, e, 0.0))
        at = jnp.full((8, 128), row)
        parts = {}
        total = values[0]
        parts[0] = values[0]
        for d in range(1, ROWS + 1):
            parts[-d] = jnp.where(at - d >= 0, values[d], 0.0)
            parts[d] = jnp.where(at + d < n_sub * ROWS, values[d], 0.0)
            total = total + parts[-d] + parts[d]
        zero = jnp.zeros((8, 128), jnp.float32)
        for i in range(PAD):
            wtab[r, i] = zero
            wtab[r, PAD + TAPS + i] = zero
        for d in range(-ROWS, ROWS + 1):
            wtab[r, PAD + ROWS + d] = parts[d] / total
        return carry

    lax.fori_loop(0, ROWS, fill, 0)

    def fill_lon(i, carry):
        start = pl.multiple_of(i * 64, 64)
        a = lax.broadcasted_iota(jnp.int32, (64, OUT), 0) + i * 64
        b = lax.broadcasted_iota(jnp.int32, (64, OUT), 1)
        d = (a - 128 - b).astype(jnp.float32)
        f = jnp.where(jnp.abs(d) <= REACH, jnp.exp(-0.5 * (d / 4.0) ** 2) / LON_SUM, 0.0)
        hi = f.astype(jnp.bfloat16)
        f_hi[pl.ds(start, 64), :] = hi
        f_lo[pl.ds(start, 64), :] = (f - hi.astype(jnp.float32)).astype(jnp.bfloat16)
        return carry

    lax.fori_loop(0, WINDOW // 64, fill_lon, 0)

    count = ROWS * TILE

    def lon_filter():
        for t in range(3):
            for i in range(4):
                c = (256 * t - 128 + 128 * i) % LON
                v = ybuf[:, c : c + 128]
                hi = v.astype(jnp.bfloat16)
                lhs_hi[count * t : count * (t + 1), 128 * i : 128 * (i + 1)] = hi
                lhs_lo[count * t : count * (t + 1), 128 * i : 128 * (i + 1)] = (v - hi.astype(jnp.float32)).astype(
                    jnp.bfloat16
                )
        h = lhs_hi[...]
        fh = f_hi[...]
        res = jnp.dot(h, fh, preferred_element_type=jnp.float32)
        res += jnp.dot(h, f_lo[...], preferred_element_type=jnp.float32)
        res += jnp.dot(lhs_lo[...], fh, preferred_element_type=jnp.float32)
        for t in range(3):
            ybuf[:, OUT * t : OUT * (t + 1)] = res[count * t : count * (t + 1)]

    def wide(w):
        return jnp.concatenate([w] * 6, axis=1)

    def piece_slices(o):
        return 3 * (o // 2), HALF * (o % 2)

    def forward(k):
        loads["c", k].wait()
        loads["p", k].wait()
        for copy in halos["c", k]:
            copy.wait_recv()

        def row(r, carry):
            acc = wide(wtab[r, PAD]) * cbuf[k, r]
            for d in range(1, TAPS):
                acc = acc + wide(wtab[r, PAD + d]) * cbuf[k, r + d]
            ybuf[pl.ds(pl.multiple_of(r * TILE, TILE), TILE), :] = acc
            return carry

        lax.fori_loop(0, ROWS, row, 0)
        lon_filter()
        for o in range(RING):
            r0, c0 = piece_slices(o)
            part = ybuf[r0 * TILE : (r0 + 3) * TILE, c0 : c0 + HALF].reshape(3, TILE, HALF)
            prod[k, o] = part * pbuf[k, r0 : r0 + 3, :, c0 : c0 + HALF]

    f_copies, b_copies = {}, {}

    def send_f(k, t):
        src = prod.at[k, ring(4)] if t == 0 else rs_f.at[k, t - 1]
        f_copies[k, t] = launch(remote(src, rs_f.at[k, t], rsf_send.at[k, t], rsf_recv.at[k, t], ahead, s))

    def send_b(k, t):
        src = prod.at[k, ring(-3)] if t == 0 else rs_b.at[k, t - 1]
        b_copies[k, t] = launch(remote(src, rs_b.at[k, t], rsb_send.at[k, t], rsb_recv.at[k, t], behind, s))

    def stage0(k):
        forward(k)
        send_f(k, 0)
        send_b(k, 0)

    def reduce_step(k, t):
        f_copies[k, t].wait_recv()
        rs_f[k, t] = rs_f[k, t] + prod[k, ring(3 - t)]
        send_f(k, t + 1)
        if t < 2:
            b_copies[k, t].wait_recv()
            rs_b[k, t] = rs_b[k, t] + prod[k, ring(t - 2)]
            send_b(k, t + 1)

    def stage4(k):
        f_copies[k, 3].wait_recv()
        b_copies[k, 2].wait_recv()
        tot[k] = prod[k, y] + rs_f[k, 3] + rs_b[k, 2]
        halos["x", k] = launch(remote(tot.at[k], xin.at[k], x_send.at[k], x_recv.at[k], partner, s))

    weights = []

    def send_weights():
        halos["w"].wait_recv()
        for j in range(1, RING):
            dest = lax.rem(y + j, RING)
            for i, (ref, owner) in enumerate(((weight, g), (wpart, partner))):
                n = 2 * j + i
                weights.append(
                    launch(
                        remote(weight_piece(ref, dest), wbuf.at[owner], w_send.at[n], w_recv.at[n], base + dest, s)
                    )
                )
        loads["x"] = pltpu.make_async_copy(weight_piece(wpart, y), wbuf.at[partner], load_sem.at[2, 1])
        loads["x"].start()

    def take_weights():
        loads["w"].wait()
        loads["x"].wait()
        for copy in weights:
            copy.wait_recv()
        for i in range(2 * RING):
            wfull[i // 4, :, 2 * (i % 4) : 2 * (i % 4) + 2, :] = wbuf[i]

    def stage5(k):
        halos["x", k].wait_recv()
        inc[k, y] = wfull[k] * (tot[k] + xin[k])
        halos["g", k] = []
        for j in (4, 3, -3, 2, -2, 1, -1):
            i = len(halos["g", k])
            halos["g", k].append(
                launch(remote(inc.at[k, y], inc.at[k, y], ag_send.at[k, i], ag_recv.at[k, i], base + ring(j), s))
            )

    def stage6(k):
        for copy in halos["g", k]:
            copy.wait_recv()
        for o in range(RING):
            r0, c0 = piece_slices(o)
            p = inc[k, o] * pbuf[k, r0 : r0 + 3, :, c0 : c0 + HALF]
            ybuf[r0 * TILE : (r0 + 3) * TILE, c0 : c0 + HALF] = p.reshape(3 * TILE, HALF)
        lon_filter()

        def row(j, carry):
            zero = jnp.zeros((TILE, LON), jnp.float32)
            mine, lo, hi = zero, zero, zero
            for i in range(ROWS):
                p = ybuf[i * TILE : (i + 1) * TILE, :]
                lo = lo + wide(wtab[i, PAD + j - i]) * p
                mine = mine + wide(wtab[i, PAD + ROWS + j - i]) * p
                hi = hi + wide(wtab[i, PAD + 2 * ROWS + j - i]) * p
            to_l[k, j] = lo
            own[k, j] = mine
            to_r[k, j] = hi
            return carry

        lax.fori_loop(0, ROWS, row, 0)
        halos["a", k] = (
            launch(remote(to_r.at[k], from_l.at[k], a_send.at[k, 0], a_recv.at[k, 0], g, right)),
            launch(remote(to_l.at[k], from_r.at[k], a_send.at[k, 1], a_recv.at[k, 1], g, left)),
        )

    outs = []

    def stage7(k):
        for copy in halos["a", k]:
            copy.wait_recv()

        def row(r, carry):
            own[k, r] = own[k, r] + from_l[k, r] + from_r[k, r]
            return carry

        lax.fori_loop(0, ROWS, row, 0)
        copy = pltpu.make_async_copy(own.at[k], adj_out.at[:, pl.ds(k * TILE, TILE), :], out_sem.at[k])
        copy.start()
        outs.append(copy)

    def write_increment():
        chunk = lax.div(g, 4)
        j = jnp.full((3, 2, HALF), lax.rem(g, 4))
        for o in range(RING):
            r0, c0 = piece_slices(o)
            v = inc[chunk, o]
            part = v[:, 6:8]
            for i in (2, 1, 0):
                part = jnp.where(j == i, v[:, 2 * i : 2 * i + 2], part)
            incst[r0 : r0 + 3, :, c0 : c0 + HALF] = part
        copy = pltpu.make_async_copy(incst, inc_out, out_sem.at[CHUNKS])
        copy.start()
        outs.append(copy)

    events = []
    for k in range(CHUNKS):
        t = 8.5 + 6.5 * k
        events.append((t, functools.partial(stage0, k)))
        for i in range(3):
            t += 2.2
            events.append((t, functools.partial(reduce_step, k, i)))
        t += 2.2
        events.append((t, functools.partial(stage4, k)))
        t += 3.5
        if k == 0:
            events.append((t - 0.2, take_weights))
        events.append((t, functools.partial(stage5, k)))
        t += 8.0
        events.append((t, functools.partial(stage6, k)))
        t += 9.0
        events.append((t, functools.partial(stage7, k)))
    events.append((8.6, functools.partial(send_control, 2)))
    events.append((17.4, functools.partial(send_control, 3)))
    events.append((15.2, send_weights))
    last6 = 8.5 + 6.5 * (CHUNKS - 1) + 8.8 + 3.5 + 8.0
    events.append((last6 + 0.1, write_increment))
    for _, event in sorted(events, key=lambda e: e[0]):
        event()

    for copy in pending:
        copy.wait_send()
    for copy in outs:
        copy.wait()


def shards(n_sub, control, perturbation, weight, half_width):
    f32 = jnp.float32
    vmem = lambda *shape: pltpu.VMEM(shape, f32)
    dma = pltpu.SemaphoreType.DMA
    hbm = pl.BlockSpec(memory_space=pl.ANY)
    increment, adjoint = pl.pallas_call(
        functools.partial(kernel, n_sub),
        out_shape=(
            jax.ShapeDtypeStruct((ROWS, 2, LON), f32),
            jax.ShapeDtypeStruct((ROWS, CHUNKS * TILE, LON), f32),
        ),
        in_specs=[pl.BlockSpec(memory_space=pltpu.SMEM), hbm, hbm, hbm],
        out_specs=(hbm, hbm),
        scratch_shapes=[
            vmem(CHUNKS, 3 * ROWS, TILE, LON),
            vmem(CHUNKS, ROWS, TILE, LON),
            vmem(ROWS * TILE, LON),
            pltpu.VMEM((3 * ROWS * TILE, WINDOW), jnp.bfloat16),
            pltpu.VMEM((3 * ROWS * TILE, WINDOW), jnp.bfloat16),
            pltpu.VMEM((WINDOW, OUT), jnp.bfloat16),
            pltpu.VMEM((WINDOW, OUT), jnp.bfloat16),
            vmem(ROWS, 2 * PAD + TAPS, 8, 128),
            vmem(CHUNKS, RING, 3, TILE, HALF),
            vmem(CHUNKS, 4, 3, TILE, HALF),
            vmem(CHUNKS, 3, 3, TILE, HALF),
            vmem(CHUNKS, 3, TILE, HALF),
            vmem(CHUNKS, 3, TILE, HALF),
            vmem(ROWS, 2, LON),
            vmem(2 * RING, 3, 2, HALF),
            vmem(CHUNKS, 3, TILE, HALF),
            vmem(CHUNKS, RING, 3, TILE, HALF),
            vmem(CHUNKS, ROWS, TILE, LON),
            vmem(CHUNKS, ROWS, TILE, LON),
            vmem(CHUNKS, ROWS, TILE, LON),
            vmem(CHUNKS, ROWS, TILE, LON),
            vmem(CHUNKS, ROWS, TILE, LON),
            vmem(ROWS, 2, LON),
            dma((CHUNKS, 2)),
            dma((CHUNKS, 2)),
            dma((3, CHUNKS)),
            dma((CHUNKS, 4)),
            dma((CHUNKS, 4)),
            dma((CHUNKS, 3)),
            dma((CHUNKS, 3)),
            dma((CHUNKS,)),
            dma((CHUNKS,)),
            dma((CHUNKS, 7)),
            dma((CHUNKS, 7)),
            dma((CHUNKS, 2)),
            dma((CHUNKS, 2)),
            dma((2 * RING,)),
            dma((2 * RING,)),
            dma((CHUNKS + 1,)),
        ],
        compiler_params=pltpu.CompilerParams(
            collective_id=0, has_side_effects=True, vmem_limit_bytes=60 * 1024 * 1024
        ),
        name="localize",
    )(
        half_width,
        control[0].transpose(1, 0, 2),
        perturbation[0].transpose(1, 0, 2),
        weight.transpose(1, 0, 2),
    )
    return increment.transpose(1, 0, 2), adjoint.transpose(1, 0, 2)[None]


def solution(mesh):
    return jax.shard_map(
        functools.partial(shards, mesh.shape["sub"]),
        mesh=mesh,
        in_specs=(
            P("grp", None, "sub", None),
            P("grp", None, "sub", None),
            P("grp", "sub", None),
            P(),
        ),
        out_specs=(P("grp", "sub", None), P("grp", None, "sub", None)),
        check_vma=False,
    )
```

```python
import functools
import math

import jax
import jax.numpy as jnp
from jax import lax
from jax.experimental import pallas as pl
from jax.experimental.pallas import tpu as pltpu
from jax.sharding import PartitionSpec as P

MESH = pl.DeviceIdType.MESH
ROWS = 12
TILE = 8
CHUNKS = 4
LON = 768
HALF = 384
RING = 8
REACH = 12
LON_SUM = sum(math.exp(-0.5 * (d / 4.0) ** 2) for d in range(-REACH, REACH + 1))
WINDOW = 512
OUT = 256


def kernel(
    n_sub,
    hw,
    control,
    pert,
    weight,
    inc_out,
    adj_out,
    cbuf,
    pbuf,
    ybuf,
    lhs,
    lonw,
    wtab,
    prod,
    rsbuf,
    tot,
    xin,
    wpart,
    wbuf,
    wfull,
    inc,
    own,
    to_l,
    to_r,
    from_l,
    from_r,
    incst,
    c_send,
    c_recv,
    load_sem,
    rs_send,
    rs_recv,
    x_send,
    x_recv,
    ag_send,
    ag_recv,
    a_send,
    a_recv,
    w_send,
    w_recv,
    out_sem,
):
    g = lax.axis_index("grp")
    s = lax.axis_index("sub")
    y = lax.rem(g, RING)
    xh = lax.div(g, RING)
    base = xh * RING
    core = lax.rem(s, 2)
    sign = 1 - 2 * core
    left, has_left = jnp.maximum(s - 1, 0), s > 0
    right, has_right = jnp.minimum(s + 1, n_sub - 1), s < n_sub - 1

    def ring(offset):
        return lax.rem(y + sign * offset + RING, RING)

    partner = (1 - xh) * RING + y

    def remote(src, dst, ss, rs, grp, sub):
        return pltpu.make_async_remote_copy(
            src_ref=src, dst_ref=dst, send_sem=ss, recv_sem=rs, device_id=(grp, sub), device_id_type=MESH
        )

    pending = []

    def launch(copy):
        copy.start()
        pending.append(copy.wait_send)
        return copy

    class Halo:
        def __init__(self, copy, can_send, can_receive):
            self.copy, self.can_send, self.can_receive = copy, can_send, can_receive
            pl.when(can_send)(copy.start)
            pending.append(self.wait_send)

        def wait_send(self):
            pl.when(self.can_send)(self.copy.wait_send)

        def wait_recv(self):
            pl.when(self.can_receive)(self.copy.wait_recv)

    def exchange(for_right, at_left, for_left, at_right, ss, rs):
        return (
            Halo(remote(for_right, at_left, ss.at[0], rs.at[0], g, right), has_right, has_left),
            Halo(remote(for_left, at_right, ss.at[1], rs.at[1], g, left), has_left, has_right),
        )

    loads = {}
    for k in range(CHUNKS):
        levels = pl.ds(k * TILE, TILE)
        loads["c", k] = pltpu.make_async_copy(control.at[:, levels, :], cbuf.at[k, pl.ds(ROWS, ROWS)], load_sem.at[0, k])
        loads["p", k] = pltpu.make_async_copy(pert.at[:, levels, :], pbuf.at[k], load_sem.at[1, k])
        loads["c", k].start()
        loads["p", k].start()

    def weight_piece(ref, owner):
        rows = pl.ds(3 * lax.div(owner, 2), 3)
        cols = pl.ds(pl.multiple_of(lax.rem(owner, 2) * HALF, 128), HALF)
        return ref.at[rows, :, cols]

    loads["w"] = pltpu.make_async_copy(weight_piece(weight, y), wbuf.at[g], load_sem.at[2, 0])
    loads["w"].start()

    barrier = pltpu.get_barrier_semaphore()
    for grp, sub, there in ((g, left, has_left), (g, right, has_right)):
        @pl.when(there)
        def _(grp=grp, sub=sub):
            pl.semaphore_signal(barrier, inc=1, device_id=(grp, sub), device_id_type=MESH)

    for grp in (*(base + ring(j) for j in (1, -1, 2, -2)), partner):
        pl.semaphore_signal(barrier, inc=1, device_id=(grp, s), device_id_type=MESH)
    pl.semaphore_wait(barrier, 5 + has_left.astype(jnp.int32) + has_right.astype(jnp.int32))

    halos = {}

    def send_control(k):
        src = control.at[:, pl.ds(k * TILE, TILE), :]
        halos["c", k] = exchange(
            src, cbuf.at[k, pl.ds(0, ROWS)], src, cbuf.at[k, pl.ds(2 * ROWS, ROWS)], c_send.at[k], c_recv.at[k]
        )

    halos["w"] = launch(remote(weight, wpart, w_send.at[0], w_recv.at[0], partner, s))
    for k in range(CHUNKS):
        send_control(k)

    for there, at, incoming in ((has_left, 0, from_l), (has_right, 2 * ROWS, from_r)):
        @pl.when(jnp.logical_not(there))
        def _(at=at, incoming=incoming):
            def clear(k, carry):
                zero = jnp.zeros((TILE, LON), jnp.float32)
                for r in range(ROWS):
                    cbuf[k, at + r] = zero
                    incoming[k, r] = zero
                return carry

            lax.fori_loop(0, CHUNKS, clear, 0)

    def fill(r, carry):
        row = s * ROWS + r
        reach = jnp.full((8, 128), hw[row].astype(jnp.float32))
        spread = 0.5 * reach + 0.5
        inverse = 1.0 / spread
        at = jnp.full((8, 128), row)
        values = []
        total = jnp.ones((8, 128), jnp.float32)
        for d in range(ROWS + 1):
            e = jnp.where(d <= reach, jnp.exp(-0.5 * (d * inverse) ** 2), 0.0)
            values.append(e)
            if d:
                total = total + jnp.where(at - d >= 0, e, 0.0) + jnp.where(at + d < n_sub * ROWS, e, 0.0)
        scale = 1.0 / total
        for d in range(ROWS + 1):
            wtab[r, d] = values[d] * scale
        return carry

    lax.fori_loop(0, ROWS, fill, 0)

    def fill_lon(i, carry):
        start = pl.multiple_of(i * 64, 64)
        a = lax.broadcasted_iota(jnp.int32, (64, OUT), 0) + i * 64
        b = lax.broadcasted_iota(jnp.int32, (64, OUT), 1)
        d = (a - 128 - b).astype(jnp.float32)
        f = jnp.where(jnp.abs(d) <= REACH, jnp.exp(-0.5 * (d / 4.0) ** 2) / LON_SUM, 0.0)
        hi = f.astype(jnp.bfloat16)
        lonw[pl.ds(start, 64), :] = hi
        lonw[pl.ds(start + WINDOW, 64), :] = hi
        lonw[pl.ds(start + 2 * WINDOW, 64), :] = (f - hi.astype(jnp.float32)).astype(jnp.bfloat16)
        return carry

    lax.fori_loop(0, WINDOW // 64, fill_lon, 0)

    count = ROWS * TILE

    def lon_filter():
        for t in range(3):
            for i in range(4):
                c = (256 * t - 128 + 128 * i) % LON
                v = ybuf[:, c : c + 128]
                hi = v.astype(jnp.bfloat16)
                rows = slice(count * t, count * (t + 1))
                lhs[rows, 128 * i : 128 * (i + 1)] = hi
                lhs[rows, WINDOW + 128 * i : WINDOW + 128 * (i + 1)] = (v - hi.astype(jnp.float32)).astype(jnp.bfloat16)
                lhs[rows, 2 * WINDOW + 128 * i : 2 * WINDOW + 128 * (i + 1)] = hi
        for t in range(3):
            rows = slice(count * t, count * (t + 1))
            ybuf[:, OUT * t : OUT * (t + 1)] = jnp.dot(lhs[rows, :], lonw[...], preferred_element_type=jnp.float32)

    def piece_slices(o):
        return 3 * (o // 2), HALF * (o % 2)

    def forward(k):
        loads["c", k].wait()
        loads["p", k].wait()
        for copy in halos["c", k]:
            copy.wait_recv()

        def column(c, carry):
            lanes = pl.ds(pl.multiple_of(c * 128, 128), 128)
            x = [cbuf[k, i, :, lanes] for i in range(3 * ROWS)]
            for r in range(ROWS):
                acc = wtab[r, 0] * x[ROWS + r]
                for d in range(1, ROWS + 1):
                    acc = acc + wtab[r, d] * (x[ROWS + r - d] + x[ROWS + r + d])
                ybuf[r * TILE : (r + 1) * TILE, lanes] = acc
            return carry

        lax.fori_loop(0, LON // 128, column, 0)
        lon_filter()
        for o in range(RING):
            r0, c0 = piece_slices(o)
            part = ybuf[r0 * TILE : (r0 + 3) * TILE, c0 : c0 + HALF].reshape(3, TILE, HALF)
            prod[k, o] = part * pbuf[k, r0 : r0 + 3, :, c0 : c0 + HALF]

    reduce = {}

    def send_part(k, slot, src, hops):
        reduce[k, slot] = launch(
            remote(src, rsbuf.at[k, slot], rs_send.at[k, slot], rs_recv.at[k, slot], base + ring(hops), s)
        )

    def stage0(k):
        forward(k)
        for slot, (owner, hops) in enumerate(((4, 2), (3, 1), (-3, -1), (1, 1), (-1, -1))):
            send_part(k, slot, prod.at[k, ring(owner)], hops)

    def stage1(k):
        for slot in (0, 1, 2):
            reduce[k, slot].wait_recv()
        rsbuf[k, 0] = prod[k, ring(2)] + rsbuf[k, 0] + rsbuf[k, 1]
        send_part(k, 5, rsbuf.at[k, 0], 2)
        rsbuf[k, 2] = prod[k, ring(-2)] + rsbuf[k, 2]
        send_part(k, 6, rsbuf.at[k, 2], -2)

    def stage4(k):
        for slot in (3, 4, 5, 6):
            reduce[k, slot].wait_recv()
        tot[k] = prod[k, y] + rsbuf[k, 3] + rsbuf[k, 4] + rsbuf[k, 5] + rsbuf[k, 6]
        halos["x", k] = launch(remote(tot.at[k], xin.at[k], x_send.at[k], x_recv.at[k], partner, s))

    weights = []
    gather = {}

    def send_weights():
        halos["w"].wait_recv()
        for j in range(1, RING):
            dest = lax.rem(y + j, RING)
            for i, (ref, owner) in enumerate(((weight, g), (wpart, partner))):
                n = 2 * j + i
                weights.append(
                    launch(
                        remote(weight_piece(ref, dest), wbuf.at[owner], w_send.at[n], w_recv.at[n], base + dest, s)
                    )
                )
        loads["x"] = pltpu.make_async_copy(weight_piece(wpart, y), wbuf.at[partner], load_sem.at[2, 1])
        loads["x"].start()

    def take_weights():
        loads["w"].wait()
        loads["x"].wait()
        for copy in weights:
            copy.wait_recv()
        for i in range(2 * RING):
            wfull[i // 4, :, 2 * (i % 4) : 2 * (i % 4) + 2, :] = wbuf[i]

    def stage5(k):
        halos["x", k].wait_recv()
        inc[k, y] = wfull[k] * (tot[k] + xin[k])
        for slot, hops in enumerate((-2, 2, -1, 1)):
            send_inc(k, slot, y, hops)

    def send_inc(k, slot, owner, hops):
        piece = inc.at[k, owner]
        gather[k, slot] = launch(remote(piece, piece, ag_send.at[k, slot], ag_recv.at[k, slot], base + ring(hops), s))

    def stage6(k):
        gather[k, 0].wait_recv()
        send_inc(k, 4, ring(2), -2)
        send_inc(k, 5, ring(2), -1)
        gather[k, 1].wait_recv()
        send_inc(k, 6, ring(-2), 1)

    def stage8(k):
        for slot in (2, 3, 4, 5, 6):
            gather[k, slot].wait_recv()
        for o in range(RING):
            r0, c0 = piece_slices(o)
            p = inc[k, o] * pbuf[k, r0 : r0 + 3, :, c0 : c0 + HALF]
            ybuf[r0 * TILE : (r0 + 3) * TILE, c0 : c0 + HALF] = p.reshape(3 * TILE, HALF)
        lon_filter()

        def column(c, carry):
            lanes = pl.ds(pl.multiple_of(c * 128, 128), 128)
            acc = [None] * (3 * ROWS)
            for i in range(ROWS):
                p = ybuf[i * TILE : (i + 1) * TILE, lanes]
                for d in range(ROWS + 1):
                    term = wtab[i, d] * p
                    for j in {ROWS + i - d, ROWS + i + d}:
                        acc[j] = term if acc[j] is None else acc[j] + term
            for j in range(ROWS):
                to_l[k, j, :, lanes] = acc[j]
                own[k, j, :, lanes] = acc[ROWS + j]
                to_r[k, j, :, lanes] = acc[2 * ROWS + j]
            return carry

        lax.fori_loop(0, LON // 128, column, 0)
        halos["a", k] = exchange(to_r.at[k], from_l.at[k], to_l.at[k], from_r.at[k], a_send.at[k], a_recv.at[k])

    outs = []

    def stage7(k):
        for copy in halos["a", k]:
            copy.wait_recv()

        def row(r, carry):
            own[k, r] = own[k, r] + from_l[k, r] + from_r[k, r]
            return carry

        lax.fori_loop(0, ROWS, row, 0)
        copy = pltpu.make_async_copy(own.at[k], adj_out.at[:, pl.ds(k * TILE, TILE), :], out_sem.at[k])
        copy.start()
        outs.append(copy)

    def write_increment():
        chunk = lax.div(g, 4)
        j = jnp.full((3, 2, HALF), lax.rem(g, 4))
        for o in range(RING):
            r0, c0 = piece_slices(o)
            v = inc[chunk, o]
            part = v[:, 6:8]
            for i in (2, 1, 0):
                part = jnp.where(j == i, v[:, 2 * i : 2 * i + 2], part)
            incst[r0 : r0 + 3, :, c0 : c0 + HALF] = part
        copy = pltpu.make_async_copy(incst, inc_out, out_sem.at[CHUNKS])
        copy.start()
        outs.append(copy)

    events = []
    for k in range(CHUNKS):
        t = 3.1 * k
        events.append((t, functools.partial(stage0, k)))
        events.append((t + 4.0, functools.partial(stage1, k)))
        events.append((t + 8.0, functools.partial(stage4, k)))
        events.append((t + 11.7, functools.partial(stage5, k)))
        events.append((t + 15.2, functools.partial(stage6, k)))
        events.append((t + 18.7, functools.partial(stage8, k)))
        events.append((t + 30.0, functools.partial(stage7, k)))
    events.append((6.3, send_weights))
    events.append((11.6, take_weights))
    events.append((29.0, write_increment))
    for _, event in sorted(events, key=lambda e: e[0]):
        event()

    for wait_send in pending:
        wait_send()
    for copy in outs:
        copy.wait()


def finish(inc, adj, inc_out, adj_out, inc_tile, adj_tile, load_sem, store_sem):
    copies = []
    for k in range(CHUNKS):
        rows = pl.ds(3 * k, 3)
        copies.append(
            (
                pltpu.make_async_copy(adj.at[rows], adj_tile.at[rows], load_sem.at[k]),
                pltpu.make_async_copy(adj_tile.at[rows], adj_out.at[rows], store_sem.at[k]),
            )
        )
    copies.append(
        (
            pltpu.make_async_copy(inc, inc_tile, load_sem.at[CHUNKS]),
            pltpu.make_async_copy(inc_tile, inc_out, store_sem.at[CHUNKS]),
        )
    )
    for load, _ in copies:
        load.start()
    for load, store in copies:
        load.wait()
        store.start()
    for _, store in copies:
        store.wait()


def shards(n_sub, control, perturbation, weight, half_width):
    f32 = jnp.float32
    vmem = lambda *shape: pltpu.VMEM(shape, f32)
    dma = pltpu.SemaphoreType.DMA
    hbm = pl.BlockSpec(memory_space=pl.ANY)
    increment, adjoint = pl.pallas_call(
        functools.partial(kernel, n_sub),
        out_shape=(
            jax.ShapeDtypeStruct((ROWS, 2, LON), f32),
            jax.ShapeDtypeStruct((ROWS, CHUNKS * TILE, LON), f32),
        ),
        in_specs=[pl.BlockSpec(memory_space=pltpu.SMEM), hbm, hbm, hbm],
        out_specs=(hbm, hbm),
        scratch_shapes=[
            vmem(CHUNKS, 3 * ROWS, TILE, LON),
            vmem(CHUNKS, ROWS, TILE, LON),
            vmem(ROWS * TILE, LON),
            pltpu.VMEM((3 * ROWS * TILE, 3 * WINDOW), jnp.bfloat16),
            pltpu.VMEM((3 * WINDOW, OUT), jnp.bfloat16),
            vmem(ROWS, ROWS + 1, 8, 128),
            vmem(CHUNKS, RING, 3, TILE, HALF),
            vmem(CHUNKS, 7, 3, TILE, HALF),
            vmem(CHUNKS, 3, TILE, HALF),
            vmem(CHUNKS, 3, TILE, HALF),
            vmem(ROWS, 2, LON),
            vmem(2 * RING, 3, 2, HALF),
            vmem(CHUNKS, 3, TILE, HALF),
            vmem(CHUNKS, RING, 3, TILE, HALF),
            vmem(CHUNKS, ROWS, TILE, LON),
            vmem(CHUNKS, ROWS, TILE, LON),
            vmem(CHUNKS, ROWS, TILE, LON),
            vmem(CHUNKS, ROWS, TILE, LON),
            vmem(CHUNKS, ROWS, TILE, LON),
            vmem(ROWS, 2, LON),
            dma((CHUNKS, 2)),
            dma((CHUNKS, 2)),
            dma((3, CHUNKS)),
            dma((CHUNKS, 7)),
            dma((CHUNKS, 7)),
            dma((CHUNKS,)),
            dma((CHUNKS,)),
            dma((CHUNKS, 7)),
            dma((CHUNKS, 7)),
            dma((CHUNKS, 2)),
            dma((CHUNKS, 2)),
            dma((2 * RING,)),
            dma((2 * RING,)),
            dma((CHUNKS + 1,)),
        ],
        compiler_params=pltpu.CompilerParams(
            collective_id=0, has_side_effects=True, vmem_limit_bytes=60 * 1024 * 1024
        ),
        name="localize",
    )(
        half_width,
        control[0].transpose(1, 0, 2),
        perturbation[0].transpose(1, 0, 2),
        weight.transpose(1, 0, 2),
    )
    increment, adjoint = pl.pallas_call(
        finish,
        out_shape=(
            jax.ShapeDtypeStruct((ROWS, 2, LON), f32),
            jax.ShapeDtypeStruct((ROWS, CHUNKS * TILE, LON), f32),
        ),
        in_specs=[hbm, hbm],
        out_specs=(hbm, hbm),
        scratch_shapes=[
            vmem(ROWS, 2, LON),
            vmem(ROWS, CHUNKS * TILE, LON),
            dma((CHUNKS + 1,)),
            dma((CHUNKS + 1,)),
        ],
        name="finish",
    )(increment, adjoint)
    return increment.transpose(1, 0, 2), adjoint.transpose(1, 0, 2)[None]


def solution(mesh):
    return jax.shard_map(
        functools.partial(shards, mesh.shape["sub"]),
        mesh=mesh,
        in_specs=(
            P("grp", None, "sub", None),
            P("grp", None, "sub", None),
            P("grp", "sub", None),
            P(),
        ),
        out_specs=(P("grp", "sub", None), P("grp", None, "sub", None)),
        check_vma=False,
    )
```

```python
import functools
import math

import jax
import jax.numpy as jnp
from jax import lax
from jax.experimental import pallas as pl
from jax.experimental.pallas import tpu as pltpu
from jax.sharding import PartitionSpec as P

MESH = pl.DeviceIdType.MESH
ROWS = 12
TILE = 8
CHUNKS = 4
LON = 768
HALF = 384
RING = 8
REACH = 12
LON_SUM = sum(math.exp(-0.5 * (d / 4.0) ** 2) for d in range(-REACH, REACH + 1))
WINDOW = 512
OUT = 256


def kernel(
    n_sub,
    hw,
    control,
    pert,
    weight,
    inc_out,
    adj_out,
    cbuf,
    pbuf,
    ybuf,
    lhs,
    lonw,
    wtab,
    prod,
    rsbuf,
    tot,
    xin,
    wpart,
    wbuf,
    wfull,
    inc,
    own,
    to_l,
    to_r,
    from_l,
    from_r,
    incst,
    c_send,
    c_recv,
    load_sem,
    rs_send,
    rs_recv,
    x_send,
    x_recv,
    ag_send,
    ag_recv,
    a_send,
    a_recv,
    w_send,
    w_recv,
    out_sem,
):
    g = lax.axis_index("grp")
    s = lax.axis_index("sub")
    y = lax.rem(g, RING)
    xh = lax.div(g, RING)
    base = xh * RING
    left, has_left = jnp.maximum(s - 1, 0), s > 0
    right, has_right = jnp.minimum(s + 1, n_sub - 1), s < n_sub - 1

    def ring(offset):
        return lax.rem(y + offset + RING, RING)

    partner = (1 - xh) * RING + y

    def remote(src, dst, ss, rs, grp, sub):
        return pltpu.make_async_remote_copy(
            src_ref=src, dst_ref=dst, send_sem=ss, recv_sem=rs, device_id=(grp, sub), device_id_type=MESH
        )

    pending = []

    def launch(copy):
        copy.start()
        pending.append(copy.wait_send)
        return copy

    class Halo:
        def __init__(self, copy, can_send, can_receive):
            self.copy, self.can_send, self.can_receive = copy, can_send, can_receive
            pl.when(can_send)(copy.start)
            pending.append(self.wait_send)

        def wait_send(self):
            pl.when(self.can_send)(self.copy.wait_send)

        def wait_recv(self):
            pl.when(self.can_receive)(self.copy.wait_recv)

    def exchange(for_right, at_left, for_left, at_right, ss, rs):
        return (
            Halo(remote(for_right, at_left, ss.at[0], rs.at[0], g, right), has_right, has_left),
            Halo(remote(for_left, at_right, ss.at[1], rs.at[1], g, left), has_left, has_right),
        )

    loads = {}
    for k in range(CHUNKS):
        levels = pl.ds(k * TILE, TILE)
        loads["c", k] = pltpu.make_async_copy(control.at[:, levels, :], cbuf.at[k, pl.ds(ROWS, ROWS)], load_sem.at[0, k])
        loads["p", k] = pltpu.make_async_copy(pert.at[:, levels, :], pbuf.at[k], load_sem.at[1, k])
        loads["c", k].start()
        loads["p", k].start()

    def weight_piece(ref, owner):
        rows = pl.ds(3 * lax.div(owner, 2), 3)
        cols = pl.ds(pl.multiple_of(lax.rem(owner, 2) * HALF, 128), HALF)
        return ref.at[rows, :, cols]

    loads["w"] = pltpu.make_async_copy(weight_piece(weight, y), wbuf.at[g], load_sem.at[2, 0])
    loads["w"].start()

    barrier = pltpu.get_barrier_semaphore()
    for grp, sub, there in ((g, left, has_left), (g, right, has_right)):
        @pl.when(there)
        def _(grp=grp, sub=sub):
            pl.semaphore_signal(barrier, inc=1, device_id=(grp, sub), device_id_type=MESH)

    for grp in (*(base + ring(j) for j in (1, -1, 2, -2)), partner):
        pl.semaphore_signal(barrier, inc=1, device_id=(grp, s), device_id_type=MESH)
    pl.semaphore_wait(barrier, 5 + has_left.astype(jnp.int32) + has_right.astype(jnp.int32))

    halos = {}

    def send_control(k):
        src = control.at[:, pl.ds(k * TILE, TILE), :]
        halos["c", k] = exchange(
            src, cbuf.at[k, pl.ds(0, ROWS)], src, cbuf.at[k, pl.ds(2 * ROWS, ROWS)], c_send.at[k], c_recv.at[k]
        )

    send_control(0)
    halos["w"] = launch(remote(weight, wpart, w_send.at[0], w_recv.at[0], partner, s))
    for k in range(1, CHUNKS):
        send_control(k)

    for there, at, incoming in ((has_left, 0, from_l), (has_right, 2 * ROWS, from_r)):
        @pl.when(jnp.logical_not(there))
        def _(at=at, incoming=incoming):
            def clear(k, carry):
                zero = jnp.zeros((TILE, LON), jnp.float32)
                for r in range(ROWS):
                    cbuf[k, at + r] = zero
                    incoming[k, r] = zero
                return carry

            lax.fori_loop(0, CHUNKS, clear, 0)

    def fill(r, carry):
        row = s * ROWS + r
        reach = jnp.full((8, 128), hw[row].astype(jnp.float32))
        spread = 0.5 * reach + 0.5
        inverse = 1.0 / spread
        at = jnp.full((8, 128), row)
        values = []
        total = jnp.ones((8, 128), jnp.float32)
        for d in range(ROWS + 1):
            e = jnp.where(d <= reach, jnp.exp(-0.5 * (d * inverse) ** 2), 0.0)
            values.append(e)
            if d:
                total = total + jnp.where(at - d >= 0, e, 0.0) + jnp.where(at + d < n_sub * ROWS, e, 0.0)
        scale = 1.0 / total
        for d in range(ROWS + 1):
            wtab[r, d] = values[d] * scale
        return carry

    lax.fori_loop(0, ROWS, fill, 0)

    def fill_lon(i, carry):
        start = pl.multiple_of(i * 64, 64)
        a = lax.broadcasted_iota(jnp.int32, (64, OUT), 0) + i * 64
        b = lax.broadcasted_iota(jnp.int32, (64, OUT), 1)
        d = (a - 128 - b).astype(jnp.float32)
        f = jnp.where(jnp.abs(d) <= REACH, jnp.exp(-0.5 * (d / 4.0) ** 2) / LON_SUM, 0.0)
        hi = f.astype(jnp.bfloat16)
        lonw[pl.ds(start, 64), :] = hi
        lonw[pl.ds(start + WINDOW, 64), :] = hi
        lonw[pl.ds(start + 2 * WINDOW, 64), :] = (f - hi.astype(jnp.float32)).astype(jnp.bfloat16)
        return carry

    lax.fori_loop(0, WINDOW // 64, fill_lon, 0)

    count = ROWS * TILE

    def lon_filter():
        for t in range(3):
            for i in range(4):
                c = (256 * t - 128 + 128 * i) % LON
                v = ybuf[:, c : c + 128]
                hi = v.astype(jnp.bfloat16)
                rows = slice(count * t, count * (t + 1))
                lhs[rows, 128 * i : 128 * (i + 1)] = hi
                lhs[rows, WINDOW + 128 * i : WINDOW + 128 * (i + 1)] = (v - hi.astype(jnp.float32)).astype(jnp.bfloat16)
                lhs[rows, 2 * WINDOW + 128 * i : 2 * WINDOW + 128 * (i + 1)] = hi
        for t in range(3):
            rows = slice(count * t, count * (t + 1))
            ybuf[:, OUT * t : OUT * (t + 1)] = jnp.dot(lhs[rows, :], lonw[...], preferred_element_type=jnp.float32)

    def piece_slices(o):
        return 3 * (o // 2), HALF * (o % 2)

    def forward(k):
        loads["c", k].wait()
        loads["p", k].wait()
        for copy in halos["c", k]:
            copy.wait_recv()

        def column(c, carry):
            lanes = pl.ds(pl.multiple_of(c * 128, 128), 128)
            x = [cbuf[k, i, :, lanes] for i in range(3 * ROWS)]
            for r in range(ROWS):
                acc = wtab[r, 0] * x[ROWS + r]
                for d in range(1, ROWS + 1):
                    acc = acc + wtab[r, d] * (x[ROWS + r - d] + x[ROWS + r + d])
                ybuf[r * TILE : (r + 1) * TILE, lanes] = acc
            return carry

        lax.fori_loop(0, LON // 128, column, 0)
        lon_filter()
        for o in range(RING):
            r0, c0 = piece_slices(o)
            part = ybuf[r0 * TILE : (r0 + 3) * TILE, c0 : c0 + HALF].reshape(3, TILE, HALF)
            prod[k, o] = part * pbuf[k, r0 : r0 + 3, :, c0 : c0 + HALF]

    reduce = {}

    def send_part(k, slot, src, hops):
        reduce[k, slot] = launch(
            remote(src, rsbuf.at[k, slot], rs_send.at[k, slot], rs_recv.at[k, slot], base + ring(hops), s)
        )

    def stage0(k):
        forward(k)
        for slot, (owner, hops) in enumerate(((4, 2), (3, 1), (-3, -1), (1, 1), (-1, -1))):
            send_part(k, slot, prod.at[k, ring(owner)], hops)

    def stage1(k):
        for slot in (0, 1, 2):
            reduce[k, slot].wait_recv()
        rsbuf[k, 0] = prod[k, ring(2)] + rsbuf[k, 0] + rsbuf[k, 1]
        send_part(k, 5, rsbuf.at[k, 0], 2)
        rsbuf[k, 2] = prod[k, ring(-2)] + rsbuf[k, 2]
        send_part(k, 6, rsbuf.at[k, 2], -2)

    def stage4(k):
        for slot in (3, 4, 5, 6):
            reduce[k, slot].wait_recv()
        tot[k] = prod[k, y] + rsbuf[k, 3] + rsbuf[k, 4] + rsbuf[k, 5] + rsbuf[k, 6]
        halos["x", k] = launch(remote(tot.at[k], xin.at[k], x_send.at[k], x_recv.at[k], partner, s))

    weights = []
    gather = {}

    def send_weights():
        halos["w"].wait_recv()
        for j in range(1, RING):
            dest = lax.rem(y + j, RING)
            for i, (ref, owner) in enumerate(((weight, g), (wpart, partner))):
                n = 2 * j + i
                weights.append(
                    launch(
                        remote(weight_piece(ref, dest), wbuf.at[owner], w_send.at[n], w_recv.at[n], base + dest, s)
                    )
                )
        loads["x"] = pltpu.make_async_copy(weight_piece(wpart, y), wbuf.at[partner], load_sem.at[2, 1])
        loads["x"].start()

    def take_weights():
        loads["w"].wait()
        loads["x"].wait()
        for copy in weights:
            copy.wait_recv()
        for i in range(2 * RING):
            wfull[i // 4, :, 2 * (i % 4) : 2 * (i % 4) + 2, :] = wbuf[i]

    def stage5(k):
        halos["x", k].wait_recv()
        inc[k, y] = wfull[k] * (tot[k] + xin[k])
        for slot, hops in enumerate((-2, 2, -1, 1)):
            send_inc(k, slot, y, hops)

    def send_inc(k, slot, owner, hops):
        piece = inc.at[k, owner]
        gather[k, slot] = launch(remote(piece, piece, ag_send.at[k, slot], ag_recv.at[k, slot], base + ring(hops), s))

    def stage6(k):
        gather[k, 0].wait_recv()
        send_inc(k, 4, ring(2), -2)
        send_inc(k, 5, ring(2), -1)
        gather[k, 1].wait_recv()
        send_inc(k, 6, ring(-2), 1)

    def stage8(k):
        for slot in (2, 3, 4, 5, 6):
            gather[k, slot].wait_recv()
        for o in range(RING):
            r0, c0 = piece_slices(o)
            p = inc[k, o] * pbuf[k, r0 : r0 + 3, :, c0 : c0 + HALF]
            ybuf[r0 * TILE : (r0 + 3) * TILE, c0 : c0 + HALF] = p.reshape(3 * TILE, HALF)
        lon_filter()

        def column(c, carry):
            lanes = pl.ds(pl.multiple_of(c * 128, 128), 128)
            acc = [None] * (3 * ROWS)
            for i in range(ROWS):
                p = ybuf[i * TILE : (i + 1) * TILE, lanes]
                for d in range(ROWS + 1):
                    term = wtab[i, d] * p
                    for j in {ROWS + i - d, ROWS + i + d}:
                        acc[j] = term if acc[j] is None else acc[j] + term
            for j in range(ROWS):
                to_l[k, j, :, lanes] = acc[j]
                own[k, j, :, lanes] = acc[ROWS + j]
                to_r[k, j, :, lanes] = acc[2 * ROWS + j]
            return carry

        lax.fori_loop(0, LON // 128, column, 0)
        halos["a", k] = exchange(to_r.at[k], from_l.at[k], to_l.at[k], from_r.at[k], a_send.at[k], a_recv.at[k])

    outs = []

    def stage7(k):
        for copy in halos["a", k]:
            copy.wait_recv()

        def row(r, carry):
            own[k, r] = own[k, r] + from_l[k, r] + from_r[k, r]
            return carry

        lax.fori_loop(0, ROWS, row, 0)
        copy = pltpu.make_async_copy(own.at[k], adj_out.at[:, pl.ds(k * TILE, TILE), :], out_sem.at[k])
        copy.start()
        outs.append(copy)

    def write_increment():
        chunk = lax.div(g, 4)
        j = jnp.full((3, 2, HALF), lax.rem(g, 4))
        for o in range(RING):
            r0, c0 = piece_slices(o)
            v = inc[chunk, o]
            part = v[:, 6:8]
            for i in (2, 1, 0):
                part = jnp.where(j == i, v[:, 2 * i : 2 * i + 2], part)
            incst[r0 : r0 + 3, :, c0 : c0 + HALF] = part
        copy = pltpu.make_async_copy(incst, inc_out, out_sem.at[CHUNKS])
        copy.start()
        outs.append(copy)

    events = []
    for k in range(CHUNKS):
        t = 3.1 * k
        events.append((t, functools.partial(stage0, k)))
        events.append((t + 4.0, functools.partial(stage1, k)))
        events.append((t + 8.0, functools.partial(stage4, k)))
        events.append((t + 12.5, functools.partial(stage5, k)))
        events.append((t + 16.5, functools.partial(stage6, k)))
        events.append((t + 21.5, functools.partial(stage8, k)))
        events.append((60.0 + k, functools.partial(stage7, k)))
    events.append((8.1, send_weights))
    events.append((12.4, take_weights))
    events.append((59.0, write_increment))
    for _, event in sorted(events, key=lambda e: e[0]):
        event()

    for wait_send in pending:
        wait_send()
    for copy in outs:
        copy.wait()


def finish(inc, adj, inc_out, adj_out, inc_tile, adj_tile, load_sem, store_sem):
    copies = []
    for k in range(CHUNKS):
        rows = pl.ds(3 * k, 3)
        copies.append(
            (
                pltpu.make_async_copy(adj.at[rows], adj_tile.at[rows], load_sem.at[k]),
                pltpu.make_async_copy(adj_tile.at[rows], adj_out.at[rows], store_sem.at[k]),
            )
        )
    copies.append(
        (
            pltpu.make_async_copy(inc, inc_tile, load_sem.at[CHUNKS]),
            pltpu.make_async_copy(inc_tile, inc_out, store_sem.at[CHUNKS]),
        )
    )
    for load, _ in copies:
        load.start()
    for load, store in copies:
        load.wait()
        store.start()
    for _, store in copies:
        store.wait()


def shards(n_sub, control, perturbation, weight, half_width):
    f32 = jnp.float32
    vmem = lambda *shape: pltpu.VMEM(shape, f32)
    dma = pltpu.SemaphoreType.DMA
    hbm = pl.BlockSpec(memory_space=pl.ANY)
    increment, adjoint = pl.pallas_call(
        functools.partial(kernel, n_sub),
        out_shape=(
            jax.ShapeDtypeStruct((ROWS, 2, LON), f32),
            jax.ShapeDtypeStruct((ROWS, CHUNKS * TILE, LON), f32),
        ),
        in_specs=[pl.BlockSpec(memory_space=pltpu.SMEM), hbm, hbm, hbm],
        out_specs=(hbm, hbm),
        scratch_shapes=[
            vmem(CHUNKS, 3 * ROWS, TILE, LON),
            vmem(CHUNKS, ROWS, TILE, LON),
            vmem(ROWS * TILE, LON),
            pltpu.VMEM((3 * ROWS * TILE, 3 * WINDOW), jnp.bfloat16),
            pltpu.VMEM((3 * WINDOW, OUT), jnp.bfloat16),
            vmem(ROWS, ROWS + 1, 8, 128),
            vmem(CHUNKS, RING, 3, TILE, HALF),
            vmem(CHUNKS, 7, 3, TILE, HALF),
            vmem(CHUNKS, 3, TILE, HALF),
            vmem(CHUNKS, 3, TILE, HALF),
            vmem(ROWS, 2, LON),
            vmem(2 * RING, 3, 2, HALF),
            vmem(CHUNKS, 3, TILE, HALF),
            vmem(CHUNKS, RING, 3, TILE, HALF),
            vmem(CHUNKS, ROWS, TILE, LON),
            vmem(CHUNKS, ROWS, TILE, LON),
            vmem(CHUNKS, ROWS, TILE, LON),
            vmem(CHUNKS, ROWS, TILE, LON),
            vmem(CHUNKS, ROWS, TILE, LON),
            vmem(ROWS, 2, LON),
            dma((CHUNKS, 2)),
            dma((CHUNKS, 2)),
            dma((3, CHUNKS)),
            dma((CHUNKS, 7)),
            dma((CHUNKS, 7)),
            dma((CHUNKS,)),
            dma((CHUNKS,)),
            dma((CHUNKS, 7)),
            dma((CHUNKS, 7)),
            dma((CHUNKS, 2)),
            dma((CHUNKS, 2)),
            dma((2 * RING,)),
            dma((2 * RING,)),
            dma((CHUNKS + 1,)),
        ],
        compiler_params=pltpu.CompilerParams(
            collective_id=0, has_side_effects=True, vmem_limit_bytes=60 * 1024 * 1024
        ),
        name="localize",
    )(
        half_width,
        control[0].transpose(1, 0, 2),
        perturbation[0].transpose(1, 0, 2),
        weight.transpose(1, 0, 2),
    )
    increment, adjoint = pl.pallas_call(
        finish,
        out_shape=(
            jax.ShapeDtypeStruct((ROWS, 2, LON), f32),
            jax.ShapeDtypeStruct((ROWS, CHUNKS * TILE, LON), f32),
        ),
        in_specs=[hbm, hbm],
        out_specs=(hbm, hbm),
        scratch_shapes=[
            vmem(ROWS, 2, LON),
            vmem(ROWS, CHUNKS * TILE, LON),
            dma((CHUNKS + 1,)),
            dma((CHUNKS + 1,)),
        ],
        name="finish",
    )(increment, adjoint)
    return increment.transpose(1, 0, 2), adjoint.transpose(1, 0, 2)[None]


def solution(mesh):
    return jax.shard_map(
        functools.partial(shards, mesh.shape["sub"]),
        mesh=mesh,
        in_specs=(
            P("grp", None, "sub", None),
            P("grp", None, "sub", None),
            P("grp", "sub", None),
            P(),
        ),
        out_specs=(P("grp", "sub", None), P("grp", None, "sub", None)),
        check_vma=False,
    )
```

```python
import functools
import math

import jax
import jax.numpy as jnp
from jax import lax
from jax.experimental import pallas as pl
from jax.experimental.pallas import tpu as pltpu
from jax.sharding import PartitionSpec as P

MESH = pl.DeviceIdType.MESH
ROWS = 12
TILE = 8
CHUNKS = 4
LON = 768
HALF = 384
RING = 8
REACH = 12
LON_SUM = sum(math.exp(-0.5 * (d / 4.0) ** 2) for d in range(-REACH, REACH + 1))
WINDOW = 512
OUT = 256


def kernel(
    n_sub,
    hw,
    control,
    pert,
    weight,
    inc_out,
    adj_out,
    cbuf,
    pbuf,
    ybuf,
    lhs,
    lonw,
    wtab,
    prod,
    rsbuf,
    tot,
    xin,
    wpart,
    wbuf,
    wfull,
    inc,
    own,
    to_l,
    to_r,
    from_l,
    from_r,
    incst,
    c_send,
    c_recv,
    load_sem,
    rs_send,
    rs_recv,
    x_send,
    x_recv,
    ag_send,
    ag_recv,
    a_send,
    a_recv,
    w_send,
    w_recv,
    out_sem,
):
    g = lax.axis_index("grp")
    s = lax.axis_index("sub")
    y = lax.rem(g, RING)
    xh = lax.div(g, RING)
    base = xh * RING
    left, has_left = jnp.maximum(s - 1, 0), s > 0
    right, has_right = jnp.minimum(s + 1, n_sub - 1), s < n_sub - 1

    def ring(offset):
        return lax.rem(y + offset + RING, RING)

    partner = (1 - xh) * RING + y

    def remote(src, dst, ss, rs, grp, sub):
        return pltpu.make_async_remote_copy(
            src_ref=src, dst_ref=dst, send_sem=ss, recv_sem=rs, device_id=(grp, sub), device_id_type=MESH
        )

    pending = []

    def launch(copy):
        copy.start()
        pending.append(copy.wait_send)
        return copy

    class Halo:
        def __init__(self, copy, can_send, can_receive):
            self.copy, self.can_send, self.can_receive = copy, can_send, can_receive
            pl.when(can_send)(copy.start)
            pending.append(self.wait_send)

        def wait_send(self):
            pl.when(self.can_send)(self.copy.wait_send)

        def wait_recv(self):
            pl.when(self.can_receive)(self.copy.wait_recv)

    def exchange(for_right, at_left, for_left, at_right, ss, rs):
        return (
            Halo(remote(for_right, at_left, ss.at[0], rs.at[0], g, right), has_right, has_left),
            Halo(remote(for_left, at_right, ss.at[1], rs.at[1], g, left), has_left, has_right),
        )

    barrier = pltpu.get_barrier_semaphore()
    for grp, sub, there in ((g, left, has_left), (g, right, has_right)):
        @pl.when(there)
        def _(grp=grp, sub=sub):
            pl.semaphore_signal(barrier, inc=1, device_id=(grp, sub), device_id_type=MESH)

    for grp in (*(base + ring(j) for j in (1, -1, 2, -2)), partner):
        pl.semaphore_signal(barrier, inc=1, device_id=(grp, s), device_id_type=MESH)
    loads = {}
    for k in range(CHUNKS):
        levels = pl.ds(k * TILE, TILE)
        loads["c", k] = pltpu.make_async_copy(control.at[:, levels, :], cbuf.at[k, pl.ds(ROWS, ROWS)], load_sem.at[0, k])
        loads["p", k] = pltpu.make_async_copy(pert.at[:, levels, :], pbuf.at[k], load_sem.at[1, k])
        loads["c", k].start()
        loads["p", k].start()

    def weight_piece(ref, owner):
        rows = pl.ds(3 * lax.div(owner, 2), 3)
        cols = pl.ds(pl.multiple_of(lax.rem(owner, 2) * HALF, 128), HALF)
        return ref.at[rows, :, cols]

    loads["w"] = pltpu.make_async_copy(weight_piece(weight, y), wbuf.at[g], load_sem.at[2, 0])
    loads["w"].start()

    pl.semaphore_wait(barrier, 5 + has_left.astype(jnp.int32) + has_right.astype(jnp.int32))

    halos = {}

    def send_control(k):
        src = control.at[:, pl.ds(k * TILE, TILE), :]
        halos["c", k] = exchange(
            src, cbuf.at[k, pl.ds(0, ROWS)], src, cbuf.at[k, pl.ds(2 * ROWS, ROWS)], c_send.at[k], c_recv.at[k]
        )

    send_control(0)
    halos["w"] = launch(remote(weight, wpart, w_send.at[0], w_recv.at[0], partner, s))
    for k in range(1, CHUNKS):
        send_control(k)

    for there, at, incoming in ((has_left, 0, from_l), (has_right, 2 * ROWS, from_r)):
        @pl.when(jnp.logical_not(there))
        def _(at=at, incoming=incoming):
            def clear(k, carry):
                zero = jnp.zeros((TILE, LON), jnp.float32)
                for r in range(ROWS):
                    cbuf[k, at + r] = zero
                    incoming[k, r] = zero
                return carry

            lax.fori_loop(0, CHUNKS, clear, 0)

    def fill(r, carry):
        row = s * ROWS + r
        reach = jnp.full((8, 128), hw[row].astype(jnp.float32))
        spread = 0.5 * reach + 0.5
        inverse = 1.0 / spread
        at = jnp.full((8, 128), row)
        values = []
        total = jnp.ones((8, 128), jnp.float32)
        for d in range(ROWS + 1):
            e = jnp.where(d <= reach, jnp.exp(-0.5 * (d * inverse) ** 2), 0.0)
            values.append(e)
            if d:
                total = total + jnp.where(at - d >= 0, e, 0.0) + jnp.where(at + d < n_sub * ROWS, e, 0.0)
        scale = 1.0 / total
        for d in range(ROWS + 1):
            wtab[r, d] = values[d] * scale
        return carry

    lax.fori_loop(0, ROWS, fill, 0)

    def fill_lon(i, carry):
        start = pl.multiple_of(i * 64, 64)
        a = lax.broadcasted_iota(jnp.int32, (64, OUT), 0) + i * 64
        b = lax.broadcasted_iota(jnp.int32, (64, OUT), 1)
        d = (a - 128 - b).astype(jnp.float32)
        f = jnp.where(jnp.abs(d) <= REACH, jnp.exp(-0.5 * (d / 4.0) ** 2) / LON_SUM, 0.0)
        hi = f.astype(jnp.bfloat16)
        lonw[pl.ds(start, 64), :] = hi
        lonw[pl.ds(start + WINDOW, 64), :] = hi
        lonw[pl.ds(start + 2 * WINDOW, 64), :] = (f - hi.astype(jnp.float32)).astype(jnp.bfloat16)
        return carry

    lax.fori_loop(0, WINDOW // 64, fill_lon, 0)

    count = ROWS * TILE

    def lon_filter():
        for t in range(3):
            for i in range(4):
                c = (256 * t - 128 + 128 * i) % LON
                v = ybuf[:, c : c + 128]
                hi = v.astype(jnp.bfloat16)
                rows = slice(count * t, count * (t + 1))
                lhs[rows, 128 * i : 128 * (i + 1)] = hi
                lhs[rows, WINDOW + 128 * i : WINDOW + 128 * (i + 1)] = (v - hi.astype(jnp.float32)).astype(jnp.bfloat16)
                lhs[rows, 2 * WINDOW + 128 * i : 2 * WINDOW + 128 * (i + 1)] = hi
        for t in range(3):
            rows = slice(count * t, count * (t + 1))
            ybuf[:, OUT * t : OUT * (t + 1)] = jnp.dot(lhs[rows, :], lonw[...], preferred_element_type=jnp.float32)

    def piece_slices(o):
        return 3 * (o // 2), HALF * (o % 2)

    def forward(k):
        loads["c", k].wait()
        loads["p", k].wait()
        for copy in halos["c", k]:
            copy.wait_recv()

        def column(c, carry):
            lanes = pl.ds(pl.multiple_of(c * 128, 128), 128)
            x = [cbuf[k, i, :, lanes] for i in range(3 * ROWS)]
            for r in range(ROWS):
                acc = wtab[r, 0] * x[ROWS + r]
                for d in range(1, ROWS + 1):
                    acc = acc + wtab[r, d] * (x[ROWS + r - d] + x[ROWS + r + d])
                ybuf[r * TILE : (r + 1) * TILE, lanes] = acc
            return carry

        lax.fori_loop(0, LON // 128, column, 0)
        lon_filter()
        for o in range(RING):
            r0, c0 = piece_slices(o)
            part = ybuf[r0 * TILE : (r0 + 3) * TILE, c0 : c0 + HALF].reshape(3, TILE, HALF)
            prod[k, o] = part * pbuf[k, r0 : r0 + 3, :, c0 : c0 + HALF]

    reduce = {}

    def send_part(k, slot, src, hops):
        reduce[k, slot] = launch(
            remote(src, rsbuf.at[k, slot], rs_send.at[k, slot], rs_recv.at[k, slot], base + ring(hops), s)
        )

    def stage0(k):
        forward(k)
        for slot, (owner, hops) in enumerate(((4, 2), (3, 1), (-3, -1), (1, 1), (-1, -1))):
            send_part(k, slot, prod.at[k, ring(owner)], hops)

    def stage1(k):
        for slot in (0, 1, 2):
            reduce[k, slot].wait_recv()
        rsbuf[k, 0] = prod[k, ring(2)] + rsbuf[k, 0] + rsbuf[k, 1]
        send_part(k, 5, rsbuf.at[k, 0], 2)
        rsbuf[k, 2] = prod[k, ring(-2)] + rsbuf[k, 2]
        send_part(k, 6, rsbuf.at[k, 2], -2)

    def stage4(k):
        for slot in (3, 4, 5, 6):
            reduce[k, slot].wait_recv()
        tot[k] = prod[k, y] + rsbuf[k, 3] + rsbuf[k, 4] + rsbuf[k, 5] + rsbuf[k, 6]
        halos["x", k] = launch(remote(tot.at[k], xin.at[k], x_send.at[k], x_recv.at[k], partner, s))

    weights = []
    gather = {}

    def send_weights():
        halos["w"].wait_recv()
        for j in range(1, RING):
            dest = lax.rem(y + j, RING)
            for i, (ref, owner) in enumerate(((weight, g), (wpart, partner))):
                n = 2 * j + i
                weights.append(
                    launch(
                        remote(weight_piece(ref, dest), wbuf.at[owner], w_send.at[n], w_recv.at[n], base + dest, s)
                    )
                )
        loads["x"] = pltpu.make_async_copy(weight_piece(wpart, y), wbuf.at[partner], load_sem.at[2, 1])
        loads["x"].start()

    def take_weights():
        loads["w"].wait()
        loads["x"].wait()
        for copy in weights:
            copy.wait_recv()
        for i in range(2 * RING):
            wfull[i // 4, :, 2 * (i % 4) : 2 * (i % 4) + 2, :] = wbuf[i]

    def stage5(k):
        halos["x", k].wait_recv()
        inc[k, y] = wfull[k] * (tot[k] + xin[k])
        for slot, hops in enumerate((-2, 2, -1, 1)):
            send_inc(k, slot, y, hops)

    def send_inc(k, slot, owner, hops):
        piece = inc.at[k, owner]
        gather[k, slot] = launch(remote(piece, piece, ag_send.at[k, slot], ag_recv.at[k, slot], base + ring(hops), s))

    def stage6(k):
        gather[k, 0].wait_recv()
        send_inc(k, 4, ring(2), -2)
        send_inc(k, 5, ring(2), -1)
        gather[k, 1].wait_recv()
        send_inc(k, 6, ring(-2), 1)

    def stage8(k):
        for slot in (2, 3, 4, 5, 6):
            gather[k, slot].wait_recv()
        for o in range(RING):
            r0, c0 = piece_slices(o)
            p = inc[k, o] * pbuf[k, r0 : r0 + 3, :, c0 : c0 + HALF]
            ybuf[r0 * TILE : (r0 + 3) * TILE, c0 : c0 + HALF] = p.reshape(3 * TILE, HALF)
        lon_filter()

        def column(c, carry):
            lanes = pl.ds(pl.multiple_of(c * 128, 128), 128)
            acc = [None] * (3 * ROWS)
            for i in range(ROWS):
                p = ybuf[i * TILE : (i + 1) * TILE, lanes]
                for d in range(ROWS + 1):
                    term = wtab[i, d] * p
                    for j in {ROWS + i - d, ROWS + i + d}:
                        acc[j] = term if acc[j] is None else acc[j] + term
            for j in range(ROWS):
                to_l[k, j, :, lanes] = acc[j]
                own[k, j, :, lanes] = acc[ROWS + j]
                to_r[k, j, :, lanes] = acc[2 * ROWS + j]
            return carry

        lax.fori_loop(0, LON // 128, column, 0)
        halos["a", k] = exchange(to_r.at[k], from_l.at[k], to_l.at[k], from_r.at[k], a_send.at[k], a_recv.at[k])

    outs = []

    def stage7(k):
        for copy in halos["a", k]:
            copy.wait_recv()

        def row(r, carry):
            own[k, r] = own[k, r] + from_l[k, r] + from_r[k, r]
            return carry

        lax.fori_loop(0, ROWS, row, 0)
        copy = pltpu.make_async_copy(own.at[k], adj_out.at[:, pl.ds(k * TILE, TILE), :], out_sem.at[k])
        copy.start()
        outs.append(copy)

    def write_increment():
        chunk = lax.div(g, 4)
        j = jnp.full((3, 2, HALF), lax.rem(g, 4))
        for o in range(RING):
            r0, c0 = piece_slices(o)
            v = inc[chunk, o]
            part = v[:, 6:8]
            for i in (2, 1, 0):
                part = jnp.where(j == i, v[:, 2 * i : 2 * i + 2], part)
            incst[r0 : r0 + 3, :, c0 : c0 + HALF] = part
        copy = pltpu.make_async_copy(incst, inc_out, out_sem.at[CHUNKS])
        copy.start()
        outs.append(copy)

    events = []
    for k in range(CHUNKS):
        t = 3.1 * k
        events.append((t, functools.partial(stage0, k)))
        events.append((t + 4.5, functools.partial(stage1, k)))
        events.append((t + 9.0, functools.partial(stage4, k)))
        events.append((t + 13.6, functools.partial(stage5, k)))
        events.append((t + 18.0, functools.partial(stage6, k)))
        events.append((t + 22.6, functools.partial(stage8, k)))
        events.append((60.0 + k, functools.partial(stage7, k)))
    events.append((9.1, send_weights))
    events.append((13.5, take_weights))
    events.append((59.0, write_increment))
    for _, event in sorted(events, key=lambda e: e[0]):
        event()

    for wait_send in pending:
        wait_send()
    for copy in outs:
        copy.wait()


def finish(inc, adj, inc_out, adj_out, inc_tile, adj_tile, load_sem, store_sem):
    copies = []
    for k in range(CHUNKS):
        rows = pl.ds(3 * k, 3)
        copies.append(
            (
                pltpu.make_async_copy(adj.at[rows], adj_tile.at[rows], load_sem.at[k]),
                pltpu.make_async_copy(adj_tile.at[rows], adj_out.at[rows], store_sem.at[k]),
            )
        )
    copies.append(
        (
            pltpu.make_async_copy(inc, inc_tile, load_sem.at[CHUNKS]),
            pltpu.make_async_copy(inc_tile, inc_out, store_sem.at[CHUNKS]),
        )
    )
    for load, _ in copies:
        load.start()
    for load, store in copies:
        load.wait()
        store.start()
    for _, store in copies:
        store.wait()


def shards(n_sub, control, perturbation, weight, half_width):
    f32 = jnp.float32
    vmem = lambda *shape: pltpu.VMEM(shape, f32)
    dma = pltpu.SemaphoreType.DMA
    hbm = pl.BlockSpec(memory_space=pl.ANY)
    increment, adjoint = pl.pallas_call(
        functools.partial(kernel, n_sub),
        out_shape=(
            jax.ShapeDtypeStruct((ROWS, 2, LON), f32),
            jax.ShapeDtypeStruct((ROWS, CHUNKS * TILE, LON), f32),
        ),
        in_specs=[pl.BlockSpec(memory_space=pltpu.SMEM), hbm, hbm, hbm],
        out_specs=(hbm, hbm),
        scratch_shapes=[
            vmem(CHUNKS, 3 * ROWS, TILE, LON),
            vmem(CHUNKS, ROWS, TILE, LON),
            vmem(ROWS * TILE, LON),
            pltpu.VMEM((3 * ROWS * TILE, 3 * WINDOW), jnp.bfloat16),
            pltpu.VMEM((3 * WINDOW, OUT), jnp.bfloat16),
            vmem(ROWS, ROWS + 1, 8, 128),
            vmem(CHUNKS, RING, 3, TILE, HALF),
            vmem(CHUNKS, 7, 3, TILE, HALF),
            vmem(CHUNKS, 3, TILE, HALF),
            vmem(CHUNKS, 3, TILE, HALF),
            vmem(ROWS, 2, LON),
            vmem(2 * RING, 3, 2, HALF),
            vmem(CHUNKS, 3, TILE, HALF),
            vmem(CHUNKS, RING, 3, TILE, HALF),
            vmem(CHUNKS, ROWS, TILE, LON),
            vmem(CHUNKS, ROWS, TILE, LON),
            vmem(CHUNKS, ROWS, TILE, LON),
            vmem(CHUNKS, ROWS, TILE, LON),
            vmem(CHUNKS, ROWS, TILE, LON),
            vmem(ROWS, 2, LON),
            dma((CHUNKS, 2)),
            dma((CHUNKS, 2)),
            dma((3, CHUNKS)),
            dma((CHUNKS, 7)),
            dma((CHUNKS, 7)),
            dma((CHUNKS,)),
            dma((CHUNKS,)),
            dma((CHUNKS, 7)),
            dma((CHUNKS, 7)),
            dma((CHUNKS, 2)),
            dma((CHUNKS, 2)),
            dma((2 * RING,)),
            dma((2 * RING,)),
            dma((CHUNKS + 1,)),
        ],
        compiler_params=pltpu.CompilerParams(
            collective_id=0, has_side_effects=True, vmem_limit_bytes=60 * 1024 * 1024
        ),
        name="localize",
    )(
        half_width,
        control[0].transpose(1, 0, 2),
        perturbation[0].transpose(1, 0, 2),
        weight.transpose(1, 0, 2),
    )
    increment, adjoint = pl.pallas_call(
        finish,
        out_shape=(
            jax.ShapeDtypeStruct((ROWS, 2, LON), f32),
            jax.ShapeDtypeStruct((ROWS, CHUNKS * TILE, LON), f32),
        ),
        in_specs=[hbm, hbm],
        out_specs=(hbm, hbm),
        scratch_shapes=[
            vmem(ROWS, 2, LON),
            vmem(ROWS, CHUNKS * TILE, LON),
            dma((CHUNKS + 1,)),
            dma((CHUNKS + 1,)),
        ],
        name="finish",
    )(increment, adjoint)
    return increment.transpose(1, 0, 2), adjoint.transpose(1, 0, 2)[None]


def solution(mesh):
    return jax.shard_map(
        functools.partial(shards, mesh.shape["sub"]),
        mesh=mesh,
        in_specs=(
            P("grp", None, "sub", None),
            P("grp", None, "sub", None),
            P("grp", "sub", None),
            P(),
        ),
        out_specs=(P("grp", "sub", None), P("grp", None, "sub", None)),
        check_vma=False,
    )
```
